32 devices in a mesh: pipe: 4 (over y, x), ctx: 8 (over z, core).
Axes of the slice: x: 2, y: 2, z: 4, core: 2. Of those that a mesh axis runs over, the one named last changes fastest.
Arguments:
- activations: bfloat16 [4, 1024, 4096], P('pipe', 'ctx'), may hold values from -17 to 17
- gate_values: bfloat16 [4, 1024, 4096], P('pipe', 'ctx'), may hold values from -6 to 6
- out_grad: bfloat16 [4, 1024, 4096], P('pipe', 'ctx'), may hold values from -6 to 6
- filters: float32 [4, 256, 128], P('pipe'), may hold values from -0.26516503 to 0.26516503
- norm_gain: float32 [4, 4096], P('pipe'), may hold values from 0.1 to 1.9
- doc_ids: int32 [4, 1024], P('pipe'), may hold values from 0 to 7, never falling along the last dimension, each value on 1 to 256 neighbouring positions
Outputs:
- prev_grad: bfloat16 [4, 1024, 4096], P('pipe', 'ctx')
- gain_grad: float32 [4, 4096], P('pipe')
The draws below stay inside these ranges and needn't reach their ends.
Inputs may be any that keep to these rules, and one draw needn't show every extreme that they name: `doc_ids`: along each section's tokens the document number never falls; a document covers 1 to 256 tokens, and every number from 0 up is used.
All inputs are finite; a program needn't handle non-finite values.
Results may differ from the reference program's by a relative error of at most 0.0042.
Values may be sent and summed in bfloat16 or wider, within the bound.
A program may use at most 64 MiB of HBM per device.

```python
import math
import jax
import jax.numpy as jnp
import numpy as np
from jax import lax

D = 4096
GROUP = 16
TAPS = 128
TOK_DEV = 128
SECTIONS = 4
TOKENS = 1024
GROUPS = 256
N_CTX = 8


def draw_activations(key, part):
    first_key, col_key, row_key = jax.random.split(key, 3)
    shape = (SECTIONS, TOKENS, D)
    base = jnp.clip(jax.random.normal(first_key, shape, jnp.float32), -5.0, 5.0)
    columns = jnp.exp(jax.random.uniform(col_key, (SECTIONS, 1, D), jnp.float32, 0.0, math.log(10.0)))
    scales = jnp.exp(jax.random.uniform(row_key, (SECTIONS, TOKENS, 1), jnp.float32, 0.0, math.log(10.0)))
    return (base * columns * scales / 30.0).astype(jnp.bfloat16)


def block_scale(stream_key, extent, cuts, least, high):
    def one(position, blocks):
        draws = jax.random.uniform(jax.random.fold_in(jax.random.fold_in(stream_key, 6), position), (blocks,), jnp.float32, least / len(cuts), high / len(cuts))
        return jnp.repeat(jnp.exp(draws), extent[position] // blocks).reshape((-1,) + (1,) * (len(extent) - position - 1))

    loudness = one(*cuts[0])
    for cut in cuts[1:]:
        loudness = loudness * one(*cut)
    return loudness


def length_profile(number_of, total, limit, lean):
    weights = [(1 << 20) // math.isqrt(grade ** lean) + 1 for grade in range(2, number_of + 1)]
    rest, holding = total - limit - (number_of - 1), [1] * (number_of - 1)
    while rest > 0:
        candidates = [i for i in range(number_of - 1) if holding[i] < limit]
        pool, remaining = sum([weights[i] for i in candidates]), rest
        for i in candidates:
            addition = min(limit - holding[i], max(1, remaining * weights[i] // pool), rest)
            holding[i] = holding[i] + addition
            rest = rest - addition
    return np.array([limit] + holding)


def ragged_sizes(key, number_of, total, most, slope):
    if number_of == 2:
        one = jax.random.randint(key, (), max(1, total - most), min(most, total - 1) + 1)
        return jnp.stack([one, total - one])
    lengths = jnp.asarray(length_profile(number_of, total, most, slope), jnp.int32)
    twos = (number_of - 1) // 2
    donor, receiver = lengths[1:1 + 2 * twos:2], lengths[2:2 + 2 * twos:2]
    margin = jnp.minimum(donor - 1, most - receiver)
    passed = jax.random.randint(jax.random.fold_in(key, 1), (twos,), 0, 1 << 20) % (margin + 1)
    lengths = lengths.at[1:1 + 2 * twos:2].set(donor - passed).at[2:2 + 2 * twos:2].set(receiver + passed)
    return lengths[jax.random.permutation(jax.random.fold_in(key, 2), number_of)]


def noise(key, dims, width, most, cuts=(), kind=jnp.bfloat16):
    level = block_scale(key, dims, cuts, -0.22, 0.18) if cuts else 1.0
    array = jax.random.normal(key, dims, jnp.float32) * width * level
    return jnp.minimum(jnp.maximum(array, -most), most).astype(kind)


def setup_inputs(seed: int = 0) -> dict:
    key_list = jax.random.split(jax.random.key(seed), 7)
    return {
        "activations": draw_activations(jax.random.fold_in(key_list[6], 71), 0),
        "gate_values": noise(key_list[1], (SECTIONS, TOKENS, D), 1.0, 6.0, ((0, 4), (1, 8))),
        "out_grad": noise(key_list[2], (SECTIONS, TOKENS, D), 1.0, 6.0, ((0, 4), (1, 8))),
        "filters": noise(key_list[3], (SECTIONS, GROUPS, TAPS), (0.5 * TAPS ** -0.5), 0.26516503, ((0, 4),), jnp.float32),
        "norm_gain": jnp.clip(1.0 + 0.18 * jax.random.normal(key_list[4], (SECTIONS, D), jnp.float32), 0.1, 1.9),
        "doc_ids": jax.vmap(lambda own: jnp.searchsorted(jnp.cumsum(ragged_sizes(own, N_CTX, TOKENS, 2 * TOK_DEV, 0)), jnp.arange(TOKENS), side="right"))(jax.random.split(key_list[5], SECTIONS)).reshape((SECTIONS, TOKENS)).astype(jnp.int32),
    }


def tap_mix(hidden_grad, filter_row, own_ids):
    length = hidden_grad.shape[0]
    reach = TAPS - 1
    extended = jnp.concatenate([hidden_grad.astype(jnp.float32), jnp.zeros((reach, D), jnp.float32)], axis=0)
    ext_ids = jnp.concatenate([own_ids, jnp.full((reach,), -1, jnp.int32)], axis=0)
    tap_table = jnp.repeat(filter_row, GROUP, axis=0).T

    def add_tap(offset, summed):
        where_at = jnp.asarray(offset).astype(jnp.int32)
        window = lax.dynamic_slice_in_dim(extended, where_at, length, 0)
        window_ids = lax.dynamic_slice_in_dim(ext_ids, where_at, length, 0)
        weight = lax.dynamic_index_in_dim(tap_table, where_at, 0, keepdims=False)
        return summed + jnp.where((window_ids == own_ids)[:, None], window * weight, 0.0)
    return lax.fori_loop(0, TAPS, add_tap, jnp.zeros((length, D), jnp.float32))

def one_section(operands):
    activations, gate_values, out_grad, filter_row, norm_gain, doc_row = operands
    features = activations.astype(jnp.float32)
    inv_rms = lax.rsqrt(lax.optimization_barrier(jnp.mean(features * features, axis=-1, keepdims=True)) + 1e-06)
    normed = features * inv_rms
    upstream = out_grad.astype(jnp.float32)
    hidden_grad = (upstream * gate_values.astype(jnp.float32)).astype(jnp.bfloat16)
    mixed_grad = tap_mix(hidden_grad, filter_row, doc_row)
    gain_grad = lax.optimization_barrier(jnp.sum(mixed_grad * normed, axis=0))
    scaled = mixed_grad * norm_gain
    projection = lax.optimization_barrier(jnp.mean(scaled * normed, axis=-1, keepdims=True))
    input_grad = (upstream + inv_rms * (scaled - normed * projection)).astype(jnp.bfloat16)
    return (input_grad, gain_grad)

def reference(activations, gate_values, out_grad, filters, norm_gain, doc_ids):
    input_grad, gain_grad = lax.map(one_section, (activations, gate_values, out_grad, filters, norm_gain, doc_ids))
    return (jnp.roll(input_grad, -1, axis=0), gain_grad)
```

```python
import functools

import jax
import jax.numpy as jnp
from jax import lax
from jax.experimental import pallas as pl
from jax.experimental.pallas import tpu as pltpu
from jax.sharding import PartitionSpec as P

BLOCKS = 4
LANES = 128
MESH = pl.DeviceIdType.MESH


def kernel(
    n_ctx, n_pipe,
    act_hbm, gate_hbm, up_hbm, filt_ref, gain_ref, ids_ref,
    out_ref, gg_ref,
    act, gate, up, hx, halo, sent, mixed, mask, inv, gacc, gsend, gslots,
    in_sem, hs_sem, hr_sem, ps_sem, pr_sem, gs_sem, gr_sem,
):
    tokens, width = act.shape
    rows = tokens // BLOCKS
    groups, taps = filt_ref.shape
    size = width // groups
    per = LANES // size
    strips = width // LANES
    ctx = lax.axis_index("ctx")
    pipe = lax.axis_index("pipe")
    has_next = ctx < n_ctx - 1
    has_prev = ctx > 0
    behind = lax.rem(pipe + n_pipe - 1, n_pipe)
    ahead = lax.rem(pipe + 1, n_pipe)

    barrier = pltpu.get_barrier_semaphore()
    for d in range(1, n_ctx):
        pl.semaphore_signal(barrier, inc=1, device_id={"ctx": lax.rem(ctx + d, n_ctx)}, device_id_type=MESH)
    pl.semaphore_signal(barrier, inc=1, device_id={"pipe": behind}, device_id_type=MESH)
    pl.semaphore_signal(barrier, inc=1, device_id={"pipe": ahead}, device_id_type=MESH)

    def part(b):
        return pl.ds(b * rows, rows)

    loads = []
    for b in range(BLOCKS):
        loads.append([
            pltpu.make_async_copy(gate_hbm.at[part(b)], gate.at[part(b)], in_sem.at[0, b]),
            pltpu.make_async_copy(up_hbm.at[part(b)], up.at[part(b)], in_sem.at[1, b]),
        ])
    act_load = pltpu.make_async_copy(act_hbm, act, in_sem.at[2, 0])
    for pair in loads:
        for one in pair:
            one.start()
    act_load.start()

    first = pl.multiple_of(ctx * tokens, LANES)
    after = pl.multiple_of(jnp.minimum(ctx + 1, n_ctx - 1) * tokens, LANES)
    own_ids = jnp.broadcast_to(ids_ref[:, pl.ds(first, tokens)].astype(jnp.float32), (tokens, tokens))
    next_ids = jnp.broadcast_to(ids_ref[:, pl.ds(after, tokens)].astype(jnp.float32), (tokens, tokens))
    out_ids = own_ids.T
    row = lax.broadcasted_iota(jnp.int32, (tokens, tokens), 0)
    col = lax.broadcasted_iota(jnp.int32, (tokens, tokens), 1)
    live = jnp.where(has_next, 1.0, 0.0)
    own_mask = jnp.where((col >= row) & (own_ids == out_ids), 1.0, 0.0)
    next_mask = jnp.where((col < row) & (next_ids == out_ids), live, 0.0)
    mask[:, :tokens] = own_mask.astype(jnp.bfloat16)
    mask[:, tokens:] = next_mask.astype(jnp.bfloat16)
    hx[tokens:, :] = jnp.zeros((tokens, width), jnp.bfloat16)
    gacc[...] = jnp.zeros_like(gacc)

    halo_copy = [
        pltpu.make_async_remote_copy(
            src_ref=hx.at[part(b)], dst_ref=halo.at[b], send_sem=hs_sem.at[b], recv_sem=hr_sem.at[b],
            device_id={"ctx": jnp.maximum(ctx - 1, 0)}, device_id_type=MESH)
        for b in range(BLOCKS)
    ]
    pipe_copy = [
        pltpu.make_async_remote_copy(
            src_ref=sent.at[part(b)], dst_ref=out_ref.at[part(b)], send_sem=ps_sem.at[b], recv_sem=pr_sem.at[b],
            device_id={"pipe": behind}, device_id_type=MESH)
        for b in range(BLOCKS)
    ]
    gain_copy = [
        pltpu.make_async_remote_copy(
            src_ref=gsend, dst_ref=gslots.at[ctx], send_sem=gs_sem.at[d], recv_sem=gr_sem.at[d],
            device_id={"ctx": lax.rem(ctx + d, n_ctx)}, device_id_type=MESH)
        for d in range(1, n_ctx)
    ]

    for b in range(BLOCKS):
        for one in loads[b]:
            one.wait()
        hx[part(b), :] = (
            up[part(b), :].astype(jnp.float32) * gate[part(b), :].astype(jnp.float32)
        ).astype(jnp.bfloat16)
        if b == 0:
            pl.semaphore_wait(barrier, n_ctx - 1 + 2)

        @pl.when(has_prev)
        def _():
            halo_copy[b].start()

    act_load.wait()

    def squares(i, total):
        x = act[:, pl.ds(pl.multiple_of(i * LANES, LANES), LANES)].astype(jnp.float32)
        return total + x * x

    total = lax.fori_loop(0, strips, squares, jnp.zeros((tokens, LANES), jnp.float32))
    inv[...] = jnp.broadcast_to(
        lax.rsqrt(jnp.sum(total, axis=1, keepdims=True) * (1.0 / width) + 1e-06), (tokens, LANES))

    lane_group = lax.broadcasted_iota(jnp.int32, (rows, LANES), 1) // size

    for b in range(BLOCKS):
        @pl.when(has_next)
        def _():
            halo_copy[b].wait_recv()
            hx[pl.ds(tokens + b * rows, rows), :] = halo[b]

        def strip(i, dots):
            cols = pl.ds(pl.multiple_of(i * LANES, LANES), LANES)
            taps_here = filt_ref[pl.ds(pl.multiple_of(i * per, per), per), :]
            own_m = mask[part(b), :tokens]
            next_m = mask[part(b), tokens:]
            pieces = []
            for g in range(per):
                ring = pltpu.roll(
                    jnp.broadcast_to(taps_here[g:g + 1, :], (rows, taps)), b * rows, 1, stride=1, stride_axis=0
                ).astype(jnp.bfloat16)
                pieces.append(jnp.concatenate([ring * own_m, ring * next_m], axis=1))
            lhs = jnp.concatenate(pieces, axis=0)
            res = jnp.dot(lhs, hx[:, cols], preferred_element_type=jnp.float32)
            mix = res[:rows]
            for g in range(1, per):
                mix = jnp.where(lane_group == g, res[g * rows:(g + 1) * rows], mix)
            mixed[:, cols] = mix
            normed = act[part(b), cols].astype(jnp.float32) * inv[part(b), :]
            both = mix * normed
            gacc[:, cols] += jnp.sum(both.reshape(rows // 8, 8, LANES), axis=0)
            return dots + both * gain_ref[:, cols]

        dots = lax.fori_loop(0, strips, strip, jnp.zeros((rows, LANES), jnp.float32))
        if b == BLOCKS - 1:
            gsend[...] = jnp.sum(gacc[...], axis=0, keepdims=True)
            gslots[ctx] = gsend[...]
            for one in gain_copy:
                one.start()
        proj = jnp.broadcast_to(jnp.sum(dots, axis=1, keepdims=True) * (1.0 / width), (rows, LANES))

        def finish(i, _):
            cols = pl.ds(pl.multiple_of(i * LANES, LANES), LANES)
            scale = inv[part(b), :]
            normed = act[part(b), cols].astype(jnp.float32) * scale
            inner = mixed[:, cols] * gain_ref[:, cols] - normed * proj
            sent[part(b), cols] = (up[part(b), cols].astype(jnp.float32) + scale * inner).astype(jnp.bfloat16)
            return 0

        lax.fori_loop(0, strips, finish, 0)
        pipe_copy[b].start()

    for one in gain_copy:
        one.wait_recv()
    gg_ref[...] = jnp.sum(gslots[...], axis=0)
    for one in gain_copy:
        one.wait_send()
    for b in range(BLOCKS):
        @pl.when(has_prev)
        def _():
            halo_copy[b].wait_send()
    for one in pipe_copy:
        one.wait()


def solution(mesh):
    n_ctx, n_pipe = mesh.shape["ctx"], mesh.shape["pipe"]

    def on_device(activations, gate_values, out_grad, filters, norm_gain, doc_ids):
        _, tokens, width = activations.shape
        rows = tokens // BLOCKS
        anywhere = pl.BlockSpec(memory_space=pl.ANY)
        vmem = pl.BlockSpec(memory_space=pltpu.VMEM)
        bf16, f32 = jnp.bfloat16, jnp.float32
        grad, gain = pl.pallas_call(
            functools.partial(kernel, n_ctx, n_pipe),
            out_shape=(
                jax.ShapeDtypeStruct((tokens, width), bf16),
                jax.ShapeDtypeStruct((1, width), f32),
            ),
            in_specs=[anywhere] * 3 + [vmem] * 3,
            out_specs=(anywhere, vmem),
            scratch_shapes=[
                pltpu.VMEM((tokens, width), bf16),
                pltpu.VMEM((tokens, width), bf16),
                pltpu.VMEM((tokens, width), bf16),
                pltpu.VMEM((2 * tokens, width), bf16),
                pltpu.VMEM((BLOCKS, rows, width), bf16),
                pltpu.VMEM((tokens, width), bf16),
                pltpu.VMEM((rows, width), f32),
                pltpu.VMEM((tokens, 2 * tokens), bf16),
                pltpu.VMEM((tokens, LANES), f32),
                pltpu.VMEM((8, width), f32),
                pltpu.VMEM((1, width), f32),
                pltpu.VMEM((n_ctx, 1, width), f32),
                pltpu.SemaphoreType.DMA((3, BLOCKS)),
                pltpu.SemaphoreType.DMA((BLOCKS,)),
                pltpu.SemaphoreType.DMA((BLOCKS,)),
                pltpu.SemaphoreType.DMA((BLOCKS,)),
                pltpu.SemaphoreType.DMA((BLOCKS,)),
                pltpu.SemaphoreType.DMA((n_ctx,)),
                pltpu.SemaphoreType.DMA((n_ctx,)),
            ],
            compiler_params=pltpu.CompilerParams(
                collective_id=0, has_side_effects=True, vmem_limit_bytes=48 << 20
            ),
        )(activations[0], gate_values[0], out_grad[0], filters[0], norm_gain, doc_ids)
        return grad[None], gain

    return jax.shard_map(
        on_device,
        mesh=mesh,
        in_specs=(
            P("pipe", "ctx", None),
            P("pipe", "ctx", None),
            P("pipe", "ctx", None),
            P("pipe", None, None),
            P("pipe", None),
            P("pipe", None),
        ),
        out_specs=(P("pipe", "ctx", None), P("pipe", None)),
        check_vma=False,
    )
```

```python
import functools

import jax
import jax.numpy as jnp
from jax import lax
from jax.experimental import pallas as pl
from jax.experimental.pallas import tpu as pltpu
from jax.sharding import PartitionSpec as P

BLOCKS = 4
LANES = 128
MESH = pl.DeviceIdType.MESH


def kernel(
    n_ctx, n_pipe,
    act_hbm, gate_hbm, up_hbm, filt_hbm, gain_hbm, ids_hbm,
    out_ref, gg_ref,
    act, gate, up, filt_ref, gain_ref, ids_ref, hx, halo, sent, mixed, mask, inv, gacc, gsend, gslots,
    in_sem, hs_sem, hr_sem, ps_sem, pr_sem, gs_sem, gr_sem,
):
    tokens, width = act.shape
    rows = tokens // BLOCKS
    groups, taps = filt_ref.shape
    size = width // groups
    per = LANES // size
    strips = width // LANES
    ctx = lax.axis_index("ctx")
    pipe = lax.axis_index("pipe")
    has_next = ctx < n_ctx - 1
    has_prev = ctx > 0
    behind = lax.rem(pipe + n_pipe - 1, n_pipe)
    ahead = lax.rem(pipe + 1, n_pipe)

    barrier = pltpu.get_barrier_semaphore()
    for d in range(1, n_ctx):
        pl.semaphore_signal(barrier, inc=1, device_id={"ctx": lax.rem(ctx + d, n_ctx)}, device_id_type=MESH)
    pl.semaphore_signal(barrier, inc=1, device_id={"pipe": behind}, device_id_type=MESH)
    pl.semaphore_signal(barrier, inc=1, device_id={"pipe": ahead}, device_id_type=MESH)

    def part(b):
        return pl.ds(b * rows, rows)

    loads = []
    for b in range(BLOCKS):
        loads.append([
            pltpu.make_async_copy(gate_hbm.at[part(b)], gate.at[part(b)], in_sem.at[0, b]),
            pltpu.make_async_copy(up_hbm.at[part(b)], up.at[part(b)], in_sem.at[1, b]),
        ])
    ids_load = pltpu.make_async_copy(ids_hbm, ids_ref, in_sem.at[2, 1])
    late_loads = [
        pltpu.make_async_copy(act_hbm, act, in_sem.at[2, 0]),
        pltpu.make_async_copy(filt_hbm, filt_ref, in_sem.at[2, 2]),
        pltpu.make_async_copy(gain_hbm, gain_ref, in_sem.at[2, 3]),
    ]
    ids_load.start()
    for pair in loads:
        for one in pair:
            one.start()
    for one in late_loads:
        one.start()
    ids_load.wait()

    first = pl.multiple_of(ctx * tokens, LANES)
    after = pl.multiple_of(jnp.minimum(ctx + 1, n_ctx - 1) * tokens, LANES)
    own_ids = jnp.broadcast_to(ids_ref[:, pl.ds(first, tokens)].astype(jnp.float32), (tokens, tokens))
    next_ids = jnp.broadcast_to(ids_ref[:, pl.ds(after, tokens)].astype(jnp.float32), (tokens, tokens))
    out_ids = own_ids.T
    row = lax.broadcasted_iota(jnp.int32, (tokens, tokens), 0)
    col = lax.broadcasted_iota(jnp.int32, (tokens, tokens), 1)
    live = jnp.where(has_next, 1.0, 0.0)
    own_mask = jnp.where((col >= row) & (own_ids == out_ids), 1.0, 0.0)
    next_mask = jnp.where((col < row) & (next_ids == out_ids), live, 0.0)
    mask[:, :tokens] = own_mask.astype(jnp.bfloat16)
    mask[:, tokens:] = next_mask.astype(jnp.bfloat16)
    hx[tokens:, :] = jnp.zeros((tokens, width), jnp.bfloat16)
    gacc[...] = jnp.zeros_like(gacc)

    halo_copy = [
        pltpu.make_async_remote_copy(
            src_ref=hx.at[part(b)], dst_ref=halo.at[b], send_sem=hs_sem.at[b], recv_sem=hr_sem.at[b],
            device_id={"ctx": jnp.maximum(ctx - 1, 0)}, device_id_type=MESH)
        for b in range(BLOCKS)
    ]
    pipe_copy = [
        pltpu.make_async_remote_copy(
            src_ref=sent.at[part(b)], dst_ref=out_ref.at[part(b)], send_sem=ps_sem.at[b], recv_sem=pr_sem.at[b],
            device_id={"pipe": behind}, device_id_type=MESH)
        for b in range(BLOCKS)
    ]
    gain_copy = [
        pltpu.make_async_remote_copy(
            src_ref=gsend, dst_ref=gslots.at[ctx], send_sem=gs_sem.at[d], recv_sem=gr_sem.at[d],
            device_id={"ctx": lax.rem(ctx + d, n_ctx)}, device_id_type=MESH)
        for d in range(1, n_ctx)
    ]

    for b in range(BLOCKS):
        for one in loads[b]:
            one.wait()
        hx[part(b), :] = (
            up[part(b), :].astype(jnp.float32) * gate[part(b), :].astype(jnp.float32)
        ).astype(jnp.bfloat16)
        if b == 0:
            pl.semaphore_wait(barrier, n_ctx - 1 + 2)

        @pl.when(has_prev)
        def _():
            halo_copy[b].start()

    for one in late_loads:
        one.wait()

    def squares(i, total):
        x = act[:, pl.ds(pl.multiple_of(i * LANES, LANES), LANES)].astype(jnp.float32)
        return total + x * x

    total = lax.fori_loop(0, strips, squares, jnp.zeros((tokens, LANES), jnp.float32))
    inv[...] = jnp.broadcast_to(
        lax.rsqrt(jnp.sum(total, axis=1, keepdims=True) * (1.0 / width) + 1e-06), (tokens, LANES))

    lane_group = lax.broadcasted_iota(jnp.int32, (rows, LANES), 1) // size

    for b in range(BLOCKS):
        @pl.when(has_next)
        def _():
            halo_copy[b].wait_recv()
            hx[pl.ds(tokens + b * rows, rows), :] = halo[b]

        def strip(i, dots):
            cols = pl.ds(pl.multiple_of(i * LANES, LANES), LANES)
            taps_here = filt_ref[pl.ds(pl.multiple_of(i * per, per), per), :]
            own_m = mask[part(b), :tokens]
            next_m = mask[part(b), tokens:]
            pieces = []
            for g in range(per):
                ring = pltpu.roll(
                    jnp.broadcast_to(taps_here[g:g + 1, :], (rows, taps)), b * rows, 1, stride=1, stride_axis=0
                ).astype(jnp.bfloat16)
                pieces.append(jnp.concatenate([ring * own_m, ring * next_m], axis=1))
            lhs = jnp.concatenate(pieces, axis=0)
            res = jnp.dot(lhs, hx[:, cols], preferred_element_type=jnp.float32)
            mix = res[:rows]
            for g in range(1, per):
                mix = jnp.where(lane_group == g, res[g * rows:(g + 1) * rows], mix)
            mixed[:, cols] = mix
            normed = act[part(b), cols].astype(jnp.float32) * inv[part(b), :]
            both = mix * normed
            gacc[:, cols] += jnp.sum(both.reshape(rows // 8, 8, LANES), axis=0)
            return dots + both * gain_ref[:, cols]

        dots = lax.fori_loop(0, strips, strip, jnp.zeros((rows, LANES), jnp.float32), unroll=8)
        if b == BLOCKS - 1:
            gsend[...] = jnp.sum(gacc[...], axis=0, keepdims=True)
            gslots[ctx] = gsend[...]
            for one in gain_copy:
                one.start()
        proj = jnp.broadcast_to(jnp.sum(dots, axis=1, keepdims=True) * (1.0 / width), (rows, LANES))

        def finish(i, _):
            cols = pl.ds(pl.multiple_of(i * LANES, LANES), LANES)
            scale = inv[part(b), :]
            normed = act[part(b), cols].astype(jnp.float32) * scale
            inner = mixed[:, cols] * gain_ref[:, cols] - normed * proj
            sent[part(b), cols] = (up[part(b), cols].astype(jnp.float32) + scale * inner).astype(jnp.bfloat16)
            return 0

        lax.fori_loop(0, strips, finish, 0, unroll=4)
        pipe_copy[b].start()

    for one in gain_copy:
        one.wait_recv()
    gg_ref[...] = jnp.sum(gslots[...], axis=0)
    for one in gain_copy:
        one.wait_send()
    for b in range(BLOCKS):
        @pl.when(has_prev)
        def _():
            halo_copy[b].wait_send()
    for one in pipe_copy:
        one.wait()


def solution(mesh):
    n_ctx, n_pipe = mesh.shape["ctx"], mesh.shape["pipe"]

    def on_device(activations, gate_values, out_grad, filters, norm_gain, doc_ids):
        _, tokens, width = activations.shape
        rows = tokens // BLOCKS
        groups, taps = filters.shape[1:]
        anywhere = pl.BlockSpec(memory_space=pl.ANY)
        hbm = pl.BlockSpec(memory_space=pltpu.HBM)
        vmem = pl.BlockSpec(memory_space=pltpu.VMEM)
        bf16, f32 = jnp.bfloat16, jnp.float32
        grad, gain = pl.pallas_call(
            functools.partial(kernel, n_ctx, n_pipe),
            out_shape=(
                jax.ShapeDtypeStruct((tokens, width), bf16),
                jax.ShapeDtypeStruct((1, width), f32),
            ),
            in_specs=[hbm] * 6,
            out_specs=(anywhere, vmem),
            scratch_shapes=[
                pltpu.VMEM((tokens, width), bf16),
                pltpu.VMEM((tokens, width), bf16),
                pltpu.VMEM((tokens, width), bf16),
                pltpu.VMEM((groups, taps), f32),
                pltpu.VMEM(norm_gain.shape, f32),
                pltpu.VMEM(doc_ids.shape, jnp.int32),
                pltpu.VMEM((2 * tokens, width), bf16),
                pltpu.VMEM((BLOCKS, rows, width), bf16),
                pltpu.VMEM((tokens, width), bf16),
                pltpu.VMEM((rows, width), f32),
                pltpu.VMEM((tokens, 2 * tokens), bf16),
                pltpu.VMEM((tokens, LANES), f32),
                pltpu.VMEM((8, width), f32),
                pltpu.VMEM((1, width), f32),
                pltpu.VMEM((n_ctx, 1, width), f32),
                pltpu.SemaphoreType.DMA((3, BLOCKS)),
                pltpu.SemaphoreType.DMA((BLOCKS,)),
                pltpu.SemaphoreType.DMA((BLOCKS,)),
                pltpu.SemaphoreType.DMA((BLOCKS,)),
                pltpu.SemaphoreType.DMA((BLOCKS,)),
                pltpu.SemaphoreType.DMA((n_ctx,)),
                pltpu.SemaphoreType.DMA((n_ctx,)),
            ],
            compiler_params=pltpu.CompilerParams(
                collective_id=0, has_side_effects=True, vmem_limit_bytes=67043328
            ),
        )(activations[0], gate_values[0], out_grad[0], filters[0], norm_gain, doc_ids)
        return grad[None], gain

    return jax.shard_map(
        on_device,
        mesh=mesh,
        in_specs=(
            P("pipe", "ctx", None),
            P("pipe", "ctx", None),
            P("pipe", "ctx", None),
            P("pipe", None, None),
            P("pipe", None),
            P("pipe", None),
        ),
        out_specs=(P("pipe", "ctx", None), P("pipe", None)),
        check_vma=False,
    )
```

```python
import functools

import jax
import jax.numpy as jnp
from jax import lax
from jax.experimental import pallas as pl
from jax.experimental.pallas import tpu as pltpu
from jax.sharding import PartitionSpec as P

LANES = 128
MESH = pl.DeviceIdType.MESH


def cuts(tokens):
    step = tokens // 4
    edges = [0, step // 2] + list(range(step, tokens + 1, step))
    return [(a, b - a) for a, b in zip(edges[:-1], edges[1:])]


def kernel(
    n_ctx, n_pipe,
    act_hbm, gate_hbm, up_hbm, filt_hbm, gain_hbm, ids_hbm,
    out_ref, gg_ref,
    act, gate, up, filt_ref, gain_ref, ids_ref, hx, halo, sent, mixed, mask, inv, gacc, gsend, gslots,
    in_sem, hs_sem, hr_sem, ps_sem, pr_sem, gs_sem, gr_sem, wave,
):
    tokens, width = act.shape
    blocks = cuts(tokens)
    count = len(blocks)
    groups, taps = filt_ref.shape
    size = width // groups
    per = LANES // size
    strips = width // LANES
    ctx = lax.axis_index("ctx")
    pipe = lax.axis_index("pipe")
    has_next = ctx < n_ctx - 1
    has_prev = ctx > 0
    behind = lax.rem(pipe + n_pipe - 1, n_pipe)
    ahead = lax.rem(pipe + 1, n_pipe)

    barrier = pltpu.get_barrier_semaphore()
    @pl.when(has_prev)
    def _():
        pl.semaphore_signal(barrier, inc=1, device_id={"ctx": ctx - 1}, device_id_type=MESH)

    @pl.when(has_next)
    def _():
        pl.semaphore_signal(barrier, inc=1, device_id={"ctx": ctx + 1}, device_id_type=MESH)

    pl.semaphore_signal(barrier, inc=1, device_id={"pipe": behind}, device_id_type=MESH)
    pl.semaphore_signal(barrier, inc=1, device_id={"pipe": ahead}, device_id_type=MESH)

    def part(b):
        return pl.ds(*blocks[b])

    loads = []
    for b in range(count):
        loads.append([
            pltpu.make_async_copy(gate_hbm.at[part(b)], gate.at[part(b)], in_sem.at[0, b]),
            pltpu.make_async_copy(up_hbm.at[part(b)], up.at[part(b)], in_sem.at[1, b]),
        ])
    ids_load = pltpu.make_async_copy(ids_hbm, ids_ref, in_sem.at[2, 1])
    late_loads = [
        pltpu.make_async_copy(act_hbm, act, in_sem.at[2, 0]),
        pltpu.make_async_copy(filt_hbm, filt_ref, in_sem.at[2, 2]),
        pltpu.make_async_copy(gain_hbm, gain_ref, in_sem.at[2, 3]),
    ]
    for pair in loads:
        for one in pair:
            one.start()
    ids_load.start()
    for one in late_loads:
        one.start()
    halo_copy = [
        pltpu.make_async_remote_copy(
            src_ref=hx.at[part(b)], dst_ref=halo.at[part(b)], send_sem=hs_sem.at[b], recv_sem=hr_sem.at[b],
            device_id={"ctx": jnp.maximum(ctx - 1, 0)}, device_id_type=MESH)
        for b in range(count)
    ]
    pipe_copy = [
        pltpu.make_async_remote_copy(
            src_ref=sent.at[part(b)], dst_ref=out_ref.at[part(b)], send_sem=ps_sem.at[b], recv_sem=pr_sem.at[b],
            device_id={"pipe": behind}, device_id_type=MESH)
        for b in range(count)
    ]
    gain_copy = [
        pltpu.make_async_remote_copy(
            src_ref=gsend, dst_ref=gslots.at[ctx], send_sem=gs_sem.at[d], recv_sem=gr_sem.at[d],
            device_id={"ctx": lax.rem(ctx + d, n_ctx)}, device_id_type=MESH)
        for d in range(1, n_ctx)
    ]

    for b in range(count):
        for one in loads[b]:
            one.wait()
        hx[part(b), :] = (
            up[part(b), :].astype(jnp.float32) * gate[part(b), :].astype(jnp.float32)
        ).astype(jnp.bfloat16)
        if b == 0:
            pl.semaphore_wait(barrier, 2 + has_prev.astype(jnp.int32) + has_next.astype(jnp.int32))

        @pl.when(has_prev)
        def _():
            halo_copy[b].start()

    ids_load.wait()

    first = pl.multiple_of(ctx * tokens, LANES)
    after = pl.multiple_of(jnp.minimum(ctx + 1, n_ctx - 1) * tokens, LANES)
    own_ids = jnp.broadcast_to(ids_ref[:, pl.ds(first, tokens)].astype(jnp.float32), (tokens, tokens))
    next_ids = jnp.broadcast_to(ids_ref[:, pl.ds(after, tokens)].astype(jnp.float32), (tokens, tokens))
    out_ids = own_ids.T
    row = lax.broadcasted_iota(jnp.int32, (tokens, tokens), 0)
    col = lax.broadcasted_iota(jnp.int32, (tokens, tokens), 1)
    live = jnp.where(has_next, 1.0, 0.0)
    own_mask = jnp.where((col >= row) & (own_ids == out_ids), 1.0, 0.0)
    next_mask = jnp.where((col < row) & (next_ids == out_ids), live, 0.0)
    mask[:, :tokens] = own_mask.astype(jnp.bfloat16)
    mask[:, tokens:] = next_mask.astype(jnp.bfloat16)
    hx[tokens:, :] = jnp.zeros((tokens, width), jnp.bfloat16)
    gacc[...] = jnp.zeros_like(gacc)

    for one in late_loads:
        one.wait()

    def squares(i, total):
        x = act[:, pl.ds(pl.multiple_of(i * LANES, LANES), LANES)].astype(jnp.float32)
        return total + x * x

    total = lax.fori_loop(0, strips, squares, jnp.zeros((tokens, LANES), jnp.float32))
    inv[...] = jnp.broadcast_to(
        lax.rsqrt(jnp.sum(total, axis=1, keepdims=True) * (1.0 / width) + 1e-06), (tokens, LANES))

    for b in range(count):
        start, rows = blocks[b]
        lane_group = lax.broadcasted_iota(jnp.int32, (rows, LANES), 1) // size

        @pl.when(has_next)
        def _():
            halo_copy[b].wait_recv()
            hx[pl.ds(tokens + start, rows), :] = halo[part(b), :]

        def strip(i, dots):
            cols = pl.ds(pl.multiple_of(i * LANES, LANES), LANES)
            taps_here = filt_ref[pl.ds(pl.multiple_of(i * per, per), per), :]
            own_m = mask[part(b), :tokens]
            next_m = mask[part(b), tokens:]
            pieces = []
            for g in range(per):
                ring = pltpu.roll(
                    jnp.broadcast_to(taps_here[g:g + 1, :], (rows, taps)), start, 1, stride=1, stride_axis=0
                ).astype(jnp.bfloat16)
                pieces.append(jnp.concatenate([ring * own_m, ring * next_m], axis=1))
            lhs = jnp.concatenate(pieces, axis=0)
            res = jnp.dot(lhs, hx[:, cols], preferred_element_type=jnp.float32)
            mix = res[:rows]
            for g in range(1, per):
                mix = jnp.where(lane_group == g, res[g * rows:(g + 1) * rows], mix)
            mixed[:rows, cols] = mix
            normed = act[part(b), cols].astype(jnp.float32) * inv[part(b), :]
            both = mix * normed
            gacc[:, cols] += jnp.sum(both.reshape(rows // 8, 8, LANES), axis=0)
            return dots + both * gain_ref[:, cols]

        dots = lax.fori_loop(0, strips, strip, jnp.zeros((rows, LANES), jnp.float32), unroll=8)
        if b == count - 1:
            gsend[...] = jnp.sum(gacc[...], axis=0, keepdims=True)
            gslots[ctx] = gsend[...]
        proj = jnp.broadcast_to(jnp.sum(dots, axis=1, keepdims=True) * (1.0 / width), (rows, LANES))

        def finish(i, _):
            cols = pl.ds(pl.multiple_of(i * LANES, LANES), LANES)
            scale = inv[part(b), :]
            normed = act[part(b), cols].astype(jnp.float32) * scale
            inner = mixed[:rows, cols] * gain_ref[:, cols] - normed * proj
            sent[part(b), cols] = (up[part(b), cols].astype(jnp.float32) + scale * inner).astype(jnp.bfloat16)
            return 0

        lax.fori_loop(0, strips, finish, 0, unroll=4)
        pipe_copy[b].start()

    @pl.when(has_next)
    def _():
        pl.semaphore_wait(wave.at[0], 1)

    @pl.when(has_prev)
    def _():
        pl.semaphore_signal(wave.at[0], inc=1, device_id={"ctx": ctx - 1}, device_id_type=MESH)
        pl.semaphore_wait(wave.at[1], 1)

    @pl.when(has_next)
    def _():
        pl.semaphore_signal(wave.at[1], inc=1, device_id={"ctx": ctx + 1}, device_id_type=MESH)

    for one in gain_copy:
        one.start()
    for one in gain_copy:
        one.wait_recv()
    gg_ref[...] = jnp.sum(gslots[...], axis=0)
    for one in gain_copy:
        one.wait_send()
    for b in range(count):
        @pl.when(has_prev)
        def _():
            halo_copy[b].wait_send()
    for one in pipe_copy:
        one.wait()


def solution(mesh):
    n_ctx, n_pipe = mesh.shape["ctx"], mesh.shape["pipe"]

    def on_device(activations, gate_values, out_grad, filters, norm_gain, doc_ids):
        _, tokens, width = activations.shape
        count = len(cuts(tokens))
        most = max(rows for _, rows in cuts(tokens))
        groups, taps = filters.shape[1:]
        anywhere = pl.BlockSpec(memory_space=pl.ANY)
        hbm = pl.BlockSpec(memory_space=pltpu.HBM)
        vmem = pl.BlockSpec(memory_space=pltpu.VMEM)
        bf16, f32 = jnp.bfloat16, jnp.float32
        grad, gain = pl.pallas_call(
            functools.partial(kernel, n_ctx, n_pipe),
            out_shape=(
                pltpu.VMEM((tokens, width), bf16),
                pltpu.VMEM((1, width), f32),
            ),
            in_specs=[hbm] * 6,
            out_specs=(vmem, vmem),
            scratch_shapes=[
                pltpu.VMEM((tokens, width), bf16),
                pltpu.VMEM((tokens, width), bf16),
                pltpu.VMEM((tokens, width), bf16),
                pltpu.VMEM((groups, taps), f32),
                pltpu.VMEM(norm_gain.shape, f32),
                pltpu.VMEM(doc_ids.shape, jnp.int32),
                pltpu.VMEM((2 * tokens, width), bf16),
                pltpu.VMEM((tokens, width), bf16),
                pltpu.VMEM((tokens, width), bf16),
                pltpu.VMEM((most, width), f32),
                pltpu.VMEM((tokens, 2 * tokens), bf16),
                pltpu.VMEM((tokens, LANES), f32),
                pltpu.VMEM((8, width), f32),
                pltpu.VMEM((1, width), f32),
                pltpu.VMEM((n_ctx, 1, width), f32),
                pltpu.SemaphoreType.DMA((3, count)),
                pltpu.SemaphoreType.DMA((count,)),
                pltpu.SemaphoreType.DMA((count,)),
                pltpu.SemaphoreType.DMA((count,)),
                pltpu.SemaphoreType.DMA((count,)),
                pltpu.SemaphoreType.DMA((n_ctx,)),
                pltpu.SemaphoreType.DMA((n_ctx,)),
                pltpu.SemaphoreType.REGULAR((2,)),
            ],
            compiler_params=pltpu.CompilerParams(
                collective_id=0, has_side_effects=True, vmem_limit_bytes=60 << 20
            ),
        )(*[
            pltpu.with_memory_space_constraint(x, pltpu.HBM)
            for x in (activations[0], gate_values[0], out_grad[0], filters[0], norm_gain, doc_ids)
        ])
        return grad[None], gain

    return jax.shard_map(
        on_device,
        mesh=mesh,
        in_specs=(
            P("pipe", "ctx", None),
            P("pipe", "ctx", None),
            P("pipe", "ctx", None),
            P("pipe", None, None),
            P("pipe", None),
            P("pipe", None),
        ),
        out_specs=(P("pipe", "ctx", None), P("pipe", None)),
        check_vma=False,
    )
```

```python
import functools

import jax
import jax.numpy as jnp
from jax import lax
from jax.experimental import pallas as pl
from jax.experimental.pallas import tpu as pltpu
from jax.sharding import PartitionSpec as P

LANES = 128
MESH = pl.DeviceIdType.MESH


def cuts(tokens):
    step = tokens // 4
    edges = [0, step // 2] + list(range(step, tokens + 1, step))
    return [(a, b - a) for a, b in zip(edges[:-1], edges[1:])]


def kernel(
    n_ctx, n_pipe,
    act_hbm, gate_hbm, up_hbm, filt_hbm, gain_hbm, ids_hbm,
    out_ref, gg_ref,
    act, gate, up, filt_ref, gain_ref, ids_ref, hx, halo, sent, mixed, mask, inv, gacc, gsend, gslots,
    in_sem, hs_sem, hr_sem, ps_sem, pr_sem, gs_sem, gr_sem, wave,
):
    tokens, width = act.shape
    blocks = cuts(tokens)
    count = len(blocks)
    groups, taps = filt_ref.shape
    size = width // groups
    per = LANES // size
    strips = width // LANES
    ctx = lax.axis_index("ctx")
    pipe = lax.axis_index("pipe")
    has_next = ctx < n_ctx - 1
    has_prev = ctx > 0
    behind = lax.rem(pipe + n_pipe - 1, n_pipe)
    ahead = lax.rem(pipe + 1, n_pipe)

    barrier = pltpu.get_barrier_semaphore()
    @pl.when(has_prev)
    def _():
        pl.semaphore_signal(barrier, inc=1, device_id={"ctx": ctx - 1}, device_id_type=MESH)

    @pl.when(has_next)
    def _():
        pl.semaphore_signal(barrier, inc=1, device_id={"ctx": ctx + 1}, device_id_type=MESH)

    pl.semaphore_signal(barrier, inc=1, device_id={"pipe": behind}, device_id_type=MESH)
    pl.semaphore_signal(barrier, inc=1, device_id={"pipe": ahead}, device_id_type=MESH)

    def part(b):
        return pl.ds(*blocks[b])

    loads = []
    for b in range(count):
        loads.append([
            pltpu.make_async_copy(gate_hbm.at[part(b)], gate.at[part(b)], in_sem.at[0, b]),
            pltpu.make_async_copy(up_hbm.at[part(b)], up.at[part(b)], in_sem.at[1, b]),
        ])
    ids_load = pltpu.make_async_copy(ids_hbm, ids_ref, in_sem.at[2, 1])
    late_loads = [
        pltpu.make_async_copy(act_hbm, act, in_sem.at[2, 0]),
        pltpu.make_async_copy(filt_hbm, filt_ref, in_sem.at[2, 2]),
        pltpu.make_async_copy(gain_hbm, gain_ref, in_sem.at[2, 3]),
    ]
    for pair in loads:
        for one in pair:
            one.start()
    ids_load.start()
    for one in late_loads:
        one.start()
    halo_copy = [
        pltpu.make_async_remote_copy(
            src_ref=hx.at[part(b)], dst_ref=halo.at[part(b)], send_sem=hs_sem.at[b], recv_sem=hr_sem.at[b],
            device_id={"ctx": jnp.maximum(ctx - 1, 0)}, device_id_type=MESH)
        for b in range(count)
    ]
    pipe_copy = [
        pltpu.make_async_remote_copy(
            src_ref=sent.at[part(b)], dst_ref=out_ref.at[part(b)], send_sem=ps_sem.at[b], recv_sem=pr_sem.at[b],
            device_id={"pipe": behind}, device_id_type=MESH)
        for b in range(count)
    ]
    gain_copy = [
        pltpu.make_async_remote_copy(
            src_ref=gsend, dst_ref=gslots.at[ctx], send_sem=gs_sem.at[d], recv_sem=gr_sem.at[d],
            device_id={"ctx": lax.rem(ctx + d, n_ctx)}, device_id_type=MESH)
        for d in range(1, n_ctx)
    ]

    for b in range(count):
        for one in loads[b]:
            one.wait()
        hx[part(b), :] = (
            up[part(b), :].astype(jnp.float32) * gate[part(b), :].astype(jnp.float32)
        ).astype(jnp.bfloat16)
        if b == 0:
            pl.semaphore_wait(barrier, 2 + has_prev.astype(jnp.int32) + has_next.astype(jnp.int32))

        @pl.when(has_prev)
        def _():
            halo_copy[b].start()

    ids_load.wait()

    first = pl.multiple_of(ctx * tokens, LANES)
    after = pl.multiple_of(jnp.minimum(ctx + 1, n_ctx - 1) * tokens, LANES)
    own_ids = jnp.broadcast_to(ids_ref[:, pl.ds(first, tokens)].astype(jnp.float32), (tokens, tokens))
    next_ids = jnp.broadcast_to(ids_ref[:, pl.ds(after, tokens)].astype(jnp.float32), (tokens, tokens))
    out_ids = own_ids.T
    row = lax.broadcasted_iota(jnp.int32, (tokens, tokens), 0)
    col = lax.broadcasted_iota(jnp.int32, (tokens, tokens), 1)
    live = jnp.where(has_next, 1.0, 0.0)
    own_mask = jnp.where((col >= row) & (own_ids == out_ids), 1.0, 0.0)
    next_mask = jnp.where((col < row) & (next_ids == out_ids), live, 0.0)
    mask[:, :tokens] = own_mask.astype(jnp.bfloat16)
    mask[:, tokens:] = next_mask.astype(jnp.bfloat16)
    hx[tokens:, :] = jnp.zeros((tokens, width), jnp.bfloat16)
    gacc[...] = jnp.zeros_like(gacc)

    for one in late_loads:
        one.wait()

    def squares(i, total):
        x = act[:, pl.ds(pl.multiple_of(i * LANES, LANES), LANES)].astype(jnp.float32)
        return total + x * x

    total = lax.fori_loop(0, strips, squares, jnp.zeros((tokens, LANES), jnp.float32), unroll=8)
    inv[...] = jnp.broadcast_to(
        lax.rsqrt(jnp.sum(total, axis=1, keepdims=True) * (1.0 / width) + 1e-06), (tokens, LANES))

    for b in range(count):
        start, rows = blocks[b]
        lane_group = lax.broadcasted_iota(jnp.int32, (rows, LANES), 1) // size

        @pl.when(has_next)
        def _():
            halo_copy[b].wait_recv()
            hx[pl.ds(tokens + start, rows), :] = halo[part(b), :]

        def strip(i, dots):
            cols = pl.ds(pl.multiple_of(i * LANES, LANES), LANES)
            taps_here = filt_ref[pl.ds(pl.multiple_of(i * per, per), per), :]
            own_m = mask[part(b), :tokens]
            next_m = mask[part(b), tokens:]
            pieces = []
            for g in range(per):
                ring = pltpu.roll(
                    jnp.broadcast_to(taps_here[g:g + 1, :], (rows, taps)), start, 1, stride=1, stride_axis=0
                ).astype(jnp.bfloat16)
                pieces.append(jnp.concatenate([ring * own_m, ring * next_m], axis=1))
            lhs = jnp.concatenate(pieces, axis=0)
            res = jnp.dot(lhs, hx[:, cols], preferred_element_type=jnp.float32)
            mix = res[:rows]
            for g in range(1, per):
                mix = jnp.where(lane_group == g, res[g * rows:(g + 1) * rows], mix)
            mixed[:rows, cols] = mix
            normed = act[part(b), cols].astype(jnp.float32) * inv[part(b), :]
            both = mix * normed
            gacc[:, cols] += jnp.sum(both.reshape(rows // 8, 8, LANES), axis=0)
            return dots + both * gain_ref[:, cols]

        dots = lax.fori_loop(0, strips, strip, jnp.zeros((rows, LANES), jnp.float32), unroll=8)
        if b == count - 1:
            gsend[...] = jnp.sum(gacc[...], axis=0, keepdims=True)
            gslots[ctx] = gsend[...]
        proj = jnp.broadcast_to(jnp.sum(dots, axis=1, keepdims=True) * (1.0 / width), (rows, LANES))

        def finish(i, _):
            cols = pl.ds(pl.multiple_of(i * LANES, LANES), LANES)
            scale = inv[part(b), :]
            normed = act[part(b), cols].astype(jnp.float32) * scale
            inner = mixed[:rows, cols] * gain_ref[:, cols] - normed * proj
            sent[part(b), cols] = (up[part(b), cols].astype(jnp.float32) + scale * inner).astype(jnp.bfloat16)
            return 0

        lax.fori_loop(0, strips, finish, 0, unroll=4)
        pipe_copy[b].start()

    @pl.when(has_next)
    def _():
        pl.semaphore_wait(wave.at[0], 1)

    @pl.when(has_prev)
    def _():
        pl.semaphore_signal(wave.at[0], inc=1, device_id={"ctx": ctx - 1}, device_id_type=MESH)
        pl.semaphore_wait(wave.at[1], 1)

    @pl.when(has_next)
    def _():
        pl.semaphore_signal(wave.at[1], inc=1, device_id={"ctx": ctx + 1}, device_id_type=MESH)

    for one in gain_copy:
        one.start()
    for one in gain_copy:
        one.wait_recv()
    gg_ref[...] = jnp.sum(gslots[...], axis=0)
    for one in gain_copy:
        one.wait_send()
    for b in range(count):
        @pl.when(has_prev)
        def _():
            halo_copy[b].wait_send()
    for one in pipe_copy:
        one.wait()


def deliver(grad_ref, gain_ref, out_hbm, gg_hbm, sem):
    quarter = grad_ref.shape[0] // 4
    copies = [pltpu.make_async_copy(gain_ref, gg_hbm, sem.at[4])]
    for q in range(4):
        at = pl.ds(q * quarter, quarter)
        copies.append(pltpu.make_async_copy(grad_ref.at[at], out_hbm.at[at], sem.at[q]))
    for one in copies:
        one.start()
    for one in copies:
        one.wait()


def solution(mesh):
    n_ctx, n_pipe = mesh.shape["ctx"], mesh.shape["pipe"]

    def on_device(activations, gate_values, out_grad, filters, norm_gain, doc_ids):
        _, tokens, width = activations.shape
        count = len(cuts(tokens))
        most = max(rows for _, rows in cuts(tokens))
        groups, taps = filters.shape[1:]
        anywhere = pl.BlockSpec(memory_space=pl.ANY)
        hbm = pl.BlockSpec(memory_space=pltpu.HBM)
        vmem = pl.BlockSpec(memory_space=pltpu.VMEM)
        bf16, f32 = jnp.bfloat16, jnp.float32
        grad, gain = pl.pallas_call(
            functools.partial(kernel, n_ctx, n_pipe),
            out_shape=(
                pltpu.VMEM((tokens, width), bf16),
                pltpu.VMEM((1, width), f32),
            ),
            in_specs=[hbm] * 6,
            out_specs=(vmem, vmem),
            scratch_shapes=[
                pltpu.VMEM((tokens, width), bf16),
                pltpu.VMEM((tokens, width), bf16),
                pltpu.VMEM((tokens, width), bf16),
                pltpu.VMEM((groups, taps), f32),
                pltpu.VMEM(norm_gain.shape, f32),
                pltpu.VMEM(doc_ids.shape, jnp.int32),
                pltpu.VMEM((2 * tokens, width), bf16),
                pltpu.VMEM((tokens, width), bf16),
                pltpu.VMEM((tokens, width), bf16),
                pltpu.VMEM((most, width), f32),
                pltpu.VMEM((tokens, 2 * tokens), bf16),
                pltpu.VMEM((tokens, LANES), f32),
                pltpu.VMEM((8, width), f32),
                pltpu.VMEM((1, width), f32),
                pltpu.VMEM((n_ctx, 1, width), f32),
                pltpu.SemaphoreType.DMA((3, count)),
                pltpu.SemaphoreType.DMA((count,)),
                pltpu.SemaphoreType.DMA((count,)),
                pltpu.SemaphoreType.DMA((count,)),
                pltpu.SemaphoreType.DMA((count,)),
                pltpu.SemaphoreType.DMA((n_ctx,)),
                pltpu.SemaphoreType.DMA((n_ctx,)),
                pltpu.SemaphoreType.REGULAR((2,)),
            ],
            compiler_params=pltpu.CompilerParams(
                collective_id=0, has_side_effects=True, vmem_limit_bytes=60 << 20
            ),
        )(*[
            pltpu.with_memory_space_constraint(x, pltpu.HBM)
            for x in (activations[0], gate_values[0], out_grad[0], filters[0], norm_gain, doc_ids)
        ])
        grad, gain = pl.pallas_call(
            deliver,
            out_shape=(
                jax.ShapeDtypeStruct((tokens, width), bf16),
                jax.ShapeDtypeStruct((1, width), f32),
            ),
            in_specs=[vmem] * 2,
            out_specs=[hbm] * 2,
            scratch_shapes=[pltpu.SemaphoreType.DMA((5,))],
            compiler_params=pltpu.CompilerParams(vmem_limit_bytes=1 << 20),
        )(*[pltpu.with_memory_space_constraint(x, pltpu.VMEM) for x in (grad, gain)])
        return grad[None], gain

    return jax.shard_map(
        on_device,
        mesh=mesh,
        in_specs=(
            P("pipe", "ctx", None),
            P("pipe", "ctx", None),
            P("pipe", "ctx", None),
            P("pipe", None, None),
            P("pipe", None),
            P("pipe", None),
        ),
        out_specs=(P("pipe", "ctx", None), P("pipe", None)),
        check_vma=False,
    )
```

```python
import functools

import jax
import jax.numpy as jnp
from jax import lax
from jax.experimental import pallas as pl
from jax.experimental.pallas import tpu as pltpu
from jax.sharding import PartitionSpec as P

LANES = 128
MESH = pl.DeviceIdType.MESH


def cuts(tokens):
    step = tokens // 4
    edges = [0, step // 2] + list(range(step, tokens + 1, step))
    return [(a, b - a) for a, b in zip(edges[:-1], edges[1:])]


def kernel(
    n_ctx, n_pipe,
    act_hbm, gate_hbm, up_hbm, filt_hbm, gain_hbm, ids_hbm,
    out_ref, gg_ref,
    act, gate, up, filt_ref, gain_ref, ids_ref, hx, halo, sent, mixed, mask, inv, gacc, gsend, gslots,
    in_sem, hs_sem, hr_sem, ps_sem, pr_sem, gs_sem, gr_sem, wave,
):
    tokens, width = act.shape
    blocks = cuts(tokens)
    count = len(blocks)
    groups, taps = filt_ref.shape
    size = width // groups
    per = LANES // size
    strips = width // LANES
    ctx = lax.axis_index("ctx")
    pipe = lax.axis_index("pipe")
    has_next = ctx < n_ctx - 1
    has_prev = ctx > 0
    behind = lax.rem(pipe + n_pipe - 1, n_pipe)
    ahead = lax.rem(pipe + 1, n_pipe)

    barrier = pltpu.get_barrier_semaphore()
    @pl.when(has_prev)
    def _():
        pl.semaphore_signal(barrier, inc=1, device_id={"ctx": ctx - 1}, device_id_type=MESH)

    @pl.when(has_next)
    def _():
        pl.semaphore_signal(barrier, inc=1, device_id={"ctx": ctx + 1}, device_id_type=MESH)

    pl.semaphore_signal(barrier, inc=1, device_id={"pipe": behind}, device_id_type=MESH)
    pl.semaphore_signal(barrier, inc=1, device_id={"pipe": ahead}, device_id_type=MESH)

    def part(b):
        return pl.ds(*blocks[b])

    loads = []
    for b in range(count):
        loads.append([
            pltpu.make_async_copy(gate_hbm.at[part(b)], gate.at[part(b)], in_sem.at[0, b]),
            pltpu.make_async_copy(up_hbm.at[part(b)], up.at[part(b)], in_sem.at[1, b]),
        ])
    ids_load = pltpu.make_async_copy(ids_hbm, ids_ref, in_sem.at[2, 1])
    late_loads = [
        pltpu.make_async_copy(act_hbm, act, in_sem.at[2, 0]),
        pltpu.make_async_copy(filt_hbm, filt_ref, in_sem.at[2, 2]),
        pltpu.make_async_copy(gain_hbm, gain_ref, in_sem.at[2, 3]),
    ]
    for pair in loads:
        for one in pair:
            one.start()
    ids_load.start()
    for one in late_loads:
        one.start()
    hx[tokens:, :] = jnp.zeros((tokens, width), jnp.bfloat16)
    gacc[...] = jnp.zeros_like(gacc)

    halo_copy = [
        pltpu.make_async_remote_copy(
            src_ref=hx.at[part(b)], dst_ref=halo.at[part(b)], send_sem=hs_sem.at[b], recv_sem=hr_sem.at[b],
            device_id={"ctx": jnp.maximum(ctx - 1, 0)}, device_id_type=MESH)
        for b in range(count)
    ]
    pipe_copy = [
        pltpu.make_async_remote_copy(
            src_ref=sent.at[part(b)], dst_ref=out_ref.at[part(b)], send_sem=ps_sem.at[b], recv_sem=pr_sem.at[b],
            device_id={"pipe": behind}, device_id_type=MESH)
        for b in range(count)
    ]
    gain_copy = [
        pltpu.make_async_remote_copy(
            src_ref=gsend, dst_ref=gslots.at[ctx], send_sem=gs_sem.at[d], recv_sem=gr_sem.at[d],
            device_id={"ctx": lax.rem(ctx + d, n_ctx)}, device_id_type=MESH)
        for d in range(1, n_ctx)
    ]

    for b in range(count):
        for one in loads[b]:
            one.wait()
        hx[part(b), :] = (
            up[part(b), :].astype(jnp.float32) * gate[part(b), :].astype(jnp.float32)
        ).astype(jnp.bfloat16)
        if b == 0:
            pl.semaphore_wait(barrier, 2 + has_prev.astype(jnp.int32) + has_next.astype(jnp.int32))

        @pl.when(has_prev)
        def _():
            halo_copy[b].start()

    ids_load.wait()

    first = pl.multiple_of(ctx * tokens, LANES)
    after = pl.multiple_of(jnp.minimum(ctx + 1, n_ctx - 1) * tokens, LANES)
    own_ids = jnp.broadcast_to(ids_ref[:, pl.ds(first, tokens)].astype(jnp.float32), (tokens, tokens))
    next_ids = jnp.broadcast_to(ids_ref[:, pl.ds(after, tokens)].astype(jnp.float32), (tokens, tokens))
    out_ids = own_ids.T
    row = lax.broadcasted_iota(jnp.int32, (tokens, tokens), 0)
    col = lax.broadcasted_iota(jnp.int32, (tokens, tokens), 1)
    live = jnp.where(has_next, 1.0, 0.0)
    own_mask = jnp.where((col >= row) & (own_ids == out_ids), 1.0, 0.0)
    next_mask = jnp.where((col < row) & (next_ids == out_ids), live, 0.0)
    mask[:, :tokens] = own_mask.astype(jnp.bfloat16)
    mask[:, tokens:] = next_mask.astype(jnp.bfloat16)

    for one in late_loads:
        one.wait()

    def squares(i, total):
        x = act[:, pl.ds(pl.multiple_of(i * LANES, LANES), LANES)].astype(jnp.float32)
        return total + x * x

    total = lax.fori_loop(0, strips, squares, jnp.zeros((tokens, LANES), jnp.float32), unroll=8)
    inv[...] = jnp.broadcast_to(
        lax.rsqrt(jnp.sum(total, axis=1, keepdims=True) * (1.0 / width) + 1e-06), (tokens, LANES))

    for b in range(count):
        start, rows = blocks[b]
        lane_group = lax.broadcasted_iota(jnp.int32, (rows, LANES), 1) // size

        @pl.when(has_next)
        def _():
            halo_copy[b].wait_recv()
            hx[pl.ds(tokens + start, rows), :] = halo[part(b), :]

        def strip(i, dots):
            cols = pl.ds(pl.multiple_of(i * LANES, LANES), LANES)
            taps_here = filt_ref[pl.ds(pl.multiple_of(i * per, per), per), :]
            own_m = mask[part(b), :tokens]
            next_m = mask[part(b), tokens:]
            pieces = []
            for g in range(per):
                ring = pltpu.roll(
                    jnp.broadcast_to(taps_here[g:g + 1, :], (rows, taps)), start, 1, stride=1, stride_axis=0
                ).astype(jnp.bfloat16)
                pieces.append(jnp.concatenate([ring * own_m, ring * next_m], axis=1))
            lhs = jnp.concatenate(pieces, axis=0)
            res = jnp.dot(lhs, hx[:, cols], preferred_element_type=jnp.float32)
            mix = res[:rows]
            for g in range(1, per):
                mix = jnp.where(lane_group == g, res[g * rows:(g + 1) * rows], mix)
            mixed[:rows, cols] = mix
            normed = act[part(b), cols].astype(jnp.float32) * inv[part(b), :]
            both = mix * normed
            gacc[:, cols] += jnp.sum(both.reshape(rows // 8, 8, LANES), axis=0)
            return dots + both * gain_ref[:, cols]

        dots = lax.fori_loop(0, strips, strip, jnp.zeros((rows, LANES), jnp.float32), unroll=16)
        if b == count - 1:
            gsend[...] = jnp.sum(gacc[...], axis=0, keepdims=True)
            gslots[ctx] = gsend[...]
        proj = jnp.broadcast_to(jnp.sum(dots, axis=1, keepdims=True) * (1.0 / width), (rows, LANES))

        def finish(i, _):
            cols = pl.ds(pl.multiple_of(i * LANES, LANES), LANES)
            scale = inv[part(b), :]
            normed = act[part(b), cols].astype(jnp.float32) * scale
            inner = mixed[:rows, cols] * gain_ref[:, cols] - normed * proj
            sent[part(b), cols] = (up[part(b), cols].astype(jnp.float32) + scale * inner).astype(jnp.bfloat16)
            return 0

        lax.fori_loop(0, strips, finish, 0, unroll=4)
        pipe_copy[b].start()

    @pl.when(has_next)
    def _():
        pl.semaphore_wait(wave.at[0], 1)

    @pl.when(has_prev)
    def _():
        pl.semaphore_signal(wave.at[0], inc=1, device_id={"ctx": ctx - 1}, device_id_type=MESH)
        pl.semaphore_wait(wave.at[1], 1)

    @pl.when(has_next)
    def _():
        pl.semaphore_signal(wave.at[1], inc=1, device_id={"ctx": ctx + 1}, device_id_type=MESH)

    for one in gain_copy:
        one.start()
    for one in gain_copy:
        one.wait_recv()
    gg_ref[...] = jnp.sum(gslots[...], axis=0)
    for one in gain_copy:
        one.wait_send()
    for b in range(count):
        @pl.when(has_prev)
        def _():
            halo_copy[b].wait_send()
    for one in pipe_copy:
        one.wait()


def deliver(grad_ref, gain_ref, out_hbm, gg_hbm, sem):
    quarter = grad_ref.shape[0] // 4
    copies = [pltpu.make_async_copy(gain_ref, gg_hbm, sem.at[4])]
    for q in range(4):
        at = pl.ds(q * quarter, quarter)
        copies.append(pltpu.make_async_copy(grad_ref.at[at], out_hbm.at[at], sem.at[q]))
    for one in copies:
        one.start()
    for one in copies:
        one.wait()


def solution(mesh):
    n_ctx, n_pipe = mesh.shape["ctx"], mesh.shape["pipe"]

    def on_device(activations, gate_values, out_grad, filters, norm_gain, doc_ids):
        _, tokens, width = activations.shape
        count = len(cuts(tokens))
        most = max(rows for _, rows in cuts(tokens))
        groups, taps = filters.shape[1:]
        anywhere = pl.BlockSpec(memory_space=pl.ANY)
        hbm = pl.BlockSpec(memory_space=pltpu.HBM)
        vmem = pl.BlockSpec(memory_space=pltpu.VMEM)
        bf16, f32 = jnp.bfloat16, jnp.float32
        grad, gain = pl.pallas_call(
            functools.partial(kernel, n_ctx, n_pipe),
            out_shape=(
                pltpu.VMEM((tokens, width), bf16),
                pltpu.VMEM((1, width), f32),
            ),
            in_specs=[hbm] * 6,
            out_specs=(vmem, vmem),
            scratch_shapes=[
                pltpu.VMEM((tokens, width), bf16),
                pltpu.VMEM((tokens, width), bf16),
                pltpu.VMEM((tokens, width), bf16),
                pltpu.VMEM((groups, taps), f32),
                pltpu.VMEM(norm_gain.shape, f32),
                pltpu.VMEM(doc_ids.shape, jnp.int32),
                pltpu.VMEM((2 * tokens, width), bf16),
                pltpu.VMEM((tokens, width), bf16),
                pltpu.VMEM((tokens, width), bf16),
                pltpu.VMEM((most, width), f32),
                pltpu.VMEM((tokens, 2 * tokens), bf16),
                pltpu.VMEM((tokens, LANES), f32),
                pltpu.VMEM((8, width), f32),
                pltpu.VMEM((1, width), f32),
                pltpu.VMEM((n_ctx, 1, width), f32),
                pltpu.SemaphoreType.DMA((3, count)),
                pltpu.SemaphoreType.DMA((count,)),
                pltpu.SemaphoreType.DMA((count,)),
                pltpu.SemaphoreType.DMA((count,)),
                pltpu.SemaphoreType.DMA((count,)),
                pltpu.SemaphoreType.DMA((n_ctx,)),
                pltpu.SemaphoreType.DMA((n_ctx,)),
                pltpu.SemaphoreType.REGULAR((2,)),
            ],
            compiler_params=pltpu.CompilerParams(
                collective_id=0, has_side_effects=True, vmem_limit_bytes=60 << 20
            ),
        )(*[
            pltpu.with_memory_space_constraint(x, pltpu.HBM)
            for x in (activations[0], gate_values[0], out_grad[0], filters[0], norm_gain, doc_ids)
        ])
        grad, gain = pl.pallas_call(
            deliver,
            out_shape=(
                jax.ShapeDtypeStruct((tokens, width), bf16),
                jax.ShapeDtypeStruct((1, width), f32),
            ),
            in_specs=[vmem] * 2,
            out_specs=[hbm] * 2,
            scratch_shapes=[pltpu.SemaphoreType.DMA((5,))],
            compiler_params=pltpu.CompilerParams(vmem_limit_bytes=1 << 20),
        )(*[pltpu.with_memory_space_constraint(x, pltpu.VMEM) for x in (grad, gain)])
        return grad[None], gain

    return jax.shard_map(
        on_device,
        mesh=mesh,
        in_specs=(
            P("pipe", "ctx", None),
            P("pipe", "ctx", None),
            P("pipe", "ctx", None),
            P("pipe", None, None),
            P("pipe", None),
            P("pipe", None),
        ),
        out_specs=(P("pipe", "ctx", None), P("pipe", None)),
        check_vma=False,
    )
```

```python
import functools

import jax
import jax.numpy as jnp
from jax import lax
from jax.experimental import pallas as pl
from jax.experimental.pallas import tpu as pltpu
from jax.sharding import PartitionSpec as P

LANES = 128
MESH = pl.DeviceIdType.MESH


def cuts(tokens):
    step = tokens // 4
    edges = [0, step // 2] + list(range(step, tokens + 1, step))
    return [(a, b - a) for a, b in zip(edges[:-1], edges[1:])]


def kernel(
    n_ctx, n_pipe,
    act_hbm, gate_hbm, up_hbm, filt_hbm, gain_hbm, ids_hbm,
    out_ref, gg_ref,
    act, gate, up, filt_ref, gain_ref, ids_ref, hx, halo, sent, mixed, mask, inv, gacc, gsend, gslots,
    in_sem, hs_sem, hr_sem, ps_sem, pr_sem, gs_sem, gr_sem, wave,
):
    tokens, width = act.shape
    blocks = cuts(tokens)
    count = len(blocks)
    groups, taps = filt_ref.shape
    size = width // groups
    per = LANES // size
    strips = width // LANES
    ctx = lax.axis_index("ctx")
    pipe = lax.axis_index("pipe")
    has_next = ctx < n_ctx - 1
    has_prev = ctx > 0
    behind = lax.rem(pipe + n_pipe - 1, n_pipe)
    ahead = lax.rem(pipe + 1, n_pipe)

    barrier = pltpu.get_barrier_semaphore()
    @pl.when(has_prev)
    def _():
        pl.semaphore_signal(barrier, inc=1, device_id={"ctx": ctx - 1}, device_id_type=MESH)

    @pl.when(has_next)
    def _():
        pl.semaphore_signal(barrier, inc=1, device_id={"ctx": ctx + 1}, device_id_type=MESH)

    pl.semaphore_signal(barrier, inc=1, device_id={"pipe": behind}, device_id_type=MESH)
    pl.semaphore_signal(barrier, inc=1, device_id={"pipe": ahead}, device_id_type=MESH)

    def part(b):
        return pl.ds(*blocks[b])

    loads = []
    for b in range(count):
        loads.append([
            pltpu.make_async_copy(gate_hbm.at[part(b)], gate.at[part(b)], in_sem.at[0, b]),
            pltpu.make_async_copy(up_hbm.at[part(b)], up.at[part(b)], in_sem.at[1, b]),
        ])
    ids_load = pltpu.make_async_copy(ids_hbm, ids_ref, in_sem.at[2, 1])
    late_loads = [
        pltpu.make_async_copy(act_hbm, act, in_sem.at[2, 0]),
        pltpu.make_async_copy(filt_hbm, filt_ref, in_sem.at[2, 2]),
        pltpu.make_async_copy(gain_hbm, gain_ref, in_sem.at[2, 3]),
    ]
    for pair in loads:
        for one in pair:
            one.start()
    ids_load.start()
    for one in late_loads:
        one.start()
    hx[tokens:, :] = jnp.zeros((tokens, width), jnp.bfloat16)
    gacc[...] = jnp.zeros_like(gacc)

    halo_copy = [
        pltpu.make_async_remote_copy(
            src_ref=hx.at[part(b)], dst_ref=halo.at[part(b)], send_sem=hs_sem.at[b], recv_sem=hr_sem.at[b],
            device_id={"ctx": jnp.maximum(ctx - 1, 0)}, device_id_type=MESH)
        for b in range(count)
    ]
    pipe_copy = [
        pltpu.make_async_remote_copy(
            src_ref=sent.at[part(b)], dst_ref=out_ref.at[part(b)], send_sem=ps_sem.at[b], recv_sem=pr_sem.at[b],
            device_id={"pipe": behind}, device_id_type=MESH)
        for b in range(count)
    ]
    gain_copy = [
        pltpu.make_async_remote_copy(
            src_ref=gsend, dst_ref=gslots.at[ctx], send_sem=gs_sem.at[d], recv_sem=gr_sem.at[d],
            device_id={"ctx": lax.rem(ctx + d, n_ctx)}, device_id_type=MESH)
        for d in range(1, n_ctx)
    ]

    for b in range(count):
        for one in loads[b]:
            one.wait()
        hx[part(b), :] = (
            up[part(b), :].astype(jnp.float32) * gate[part(b), :].astype(jnp.float32)
        ).astype(jnp.bfloat16)
        if b == 0:
            pl.semaphore_wait(barrier, 2 + has_prev.astype(jnp.int32) + has_next.astype(jnp.int32))

        @pl.when(has_prev)
        def _():
            halo_copy[b].start()

    ids_load.wait()

    first = pl.multiple_of(ctx * tokens, LANES)
    after = pl.multiple_of(jnp.minimum(ctx + 1, n_ctx - 1) * tokens, LANES)
    own_ids = jnp.broadcast_to(ids_ref[:, pl.ds(first, tokens)].astype(jnp.float32), (tokens, tokens))
    next_ids = jnp.broadcast_to(ids_ref[:, pl.ds(after, tokens)].astype(jnp.float32), (tokens, tokens))
    out_ids = own_ids.T
    row = lax.broadcasted_iota(jnp.int32, (tokens, tokens), 0)
    col = lax.broadcasted_iota(jnp.int32, (tokens, tokens), 1)
    live = jnp.where(has_next, 1.0, 0.0)
    own_mask = jnp.where((col >= row) & (own_ids == out_ids), 1.0, 0.0)
    next_mask = jnp.where((col < row) & (next_ids == out_ids), live, 0.0)
    mask[:, :tokens] = own_mask.astype(jnp.bfloat16)
    mask[:, tokens:] = next_mask.astype(jnp.bfloat16)

    for one in late_loads:
        one.wait()

    for b in range(count):
        start, rows = blocks[b]
        lane_group = lax.broadcasted_iota(jnp.int32, (rows, LANES), 1) // size

        def squares(i, total):
            x = act[part(b), pl.ds(pl.multiple_of(i * LANES, LANES), LANES)].astype(jnp.float32)
            return total + x * x

        total = lax.fori_loop(0, strips, squares, jnp.zeros((rows, LANES), jnp.float32), unroll=8)
        inv[part(b), :] = jnp.broadcast_to(
            lax.rsqrt(jnp.sum(total, axis=1, keepdims=True) * (1.0 / width) + 1e-06), (rows, LANES))

        @pl.when(has_next)
        def _():
            halo_copy[b].wait_recv()
            hx[pl.ds(tokens + start, rows), :] = halo[part(b), :]

        def strip(i, dots):
            cols = pl.ds(pl.multiple_of(i * LANES, LANES), LANES)
            taps_here = filt_ref[pl.ds(pl.multiple_of(i * per, per), per), :]
            own_m = mask[part(b), :tokens]
            next_m = mask[part(b), tokens:]
            pieces = []
            for g in range(per):
                ring = pltpu.roll(
                    jnp.broadcast_to(taps_here[g:g + 1, :], (rows, taps)), start, 1, stride=1, stride_axis=0
                ).astype(jnp.bfloat16)
                pieces.append(jnp.concatenate([ring * own_m, ring * next_m], axis=1))
            lhs = jnp.concatenate(pieces, axis=0)
            res = jnp.dot(lhs, hx[:, cols], preferred_element_type=jnp.float32)
            mix = res[:rows]
            for g in range(1, per):
                mix = jnp.where(lane_group == g, res[g * rows:(g + 1) * rows], mix)
            mixed[:rows, cols] = mix
            normed = act[part(b), cols].astype(jnp.float32) * inv[part(b), :]
            both = mix * normed
            gacc[:, cols] += jnp.sum(both.reshape(rows // 8, 8, LANES), axis=0)
            return dots + both * gain_ref[:, cols]

        dots = lax.fori_loop(0, strips, strip, jnp.zeros((rows, LANES), jnp.float32), unroll=16)
        if b == count - 1:
            gsend[...] = jnp.sum(gacc[...], axis=0, keepdims=True)
            gslots[ctx] = gsend[...]
        proj = jnp.broadcast_to(jnp.sum(dots, axis=1, keepdims=True) * (1.0 / width), (rows, LANES))

        def finish(i, _):
            cols = pl.ds(pl.multiple_of(i * LANES, LANES), LANES)
            scale = inv[part(b), :]
            normed = act[part(b), cols].astype(jnp.float32) * scale
            inner = mixed[:rows, cols] * gain_ref[:, cols] - normed * proj
            sent[part(b), cols] = (up[part(b), cols].astype(jnp.float32) + scale * inner).astype(jnp.bfloat16)
            return 0

        lax.fori_loop(0, strips, finish, 0, unroll=4)
        pipe_copy[b].start()

    @pl.when(has_next)
    def _():
        pl.semaphore_wait(wave.at[0], 1)

    @pl.when(has_prev)
    def _():
        pl.semaphore_signal(wave.at[0], inc=1, device_id={"ctx": ctx - 1}, device_id_type=MESH)
        pl.semaphore_wait(wave.at[1], 1)

    @pl.when(has_next)
    def _():
        pl.semaphore_signal(wave.at[1], inc=1, device_id={"ctx": ctx + 1}, device_id_type=MESH)

    for one in gain_copy:
        one.start()
    for one in gain_copy:
        one.wait_recv()
    gg_ref[...] = jnp.sum(gslots[...], axis=0)
    for one in gain_copy:
        one.wait_send()
    for b in range(count):
        @pl.when(has_prev)
        def _():
            halo_copy[b].wait_send()
    for one in pipe_copy:
        one.wait()


def deliver(grad_ref, gain_ref, out_hbm, gg_hbm, sem):
    quarter = grad_ref.shape[0] // 4
    copies = [pltpu.make_async_copy(gain_ref, gg_hbm, sem.at[4])]
    for q in range(4):
        at = pl.ds(q * quarter, quarter)
        copies.append(pltpu.make_async_copy(grad_ref.at[at], out_hbm.at[at], sem.at[q]))
    for one in copies:
        one.start()
    for one in copies:
        one.wait()


def solution(mesh):
    n_ctx, n_pipe = mesh.shape["ctx"], mesh.shape["pipe"]

    def on_device(activations, gate_values, out_grad, filters, norm_gain, doc_ids):
        _, tokens, width = activations.shape
        count = len(cuts(tokens))
        most = max(rows for _, rows in cuts(tokens))
        groups, taps = filters.shape[1:]
        anywhere = pl.BlockSpec(memory_space=pl.ANY)
        hbm = pl.BlockSpec(memory_space=pltpu.HBM)
        vmem = pl.BlockSpec(memory_space=pltpu.VMEM)
        bf16, f32 = jnp.bfloat16, jnp.float32
        grad, gain = pl.pallas_call(
            functools.partial(kernel, n_ctx, n_pipe),
            out_shape=(
                pltpu.VMEM((tokens, width), bf16),
                pltpu.VMEM((1, width), f32),
            ),
            in_specs=[hbm] * 6,
            out_specs=(vmem, vmem),
            scratch_shapes=[
                pltpu.VMEM((tokens, width), bf16),
                pltpu.VMEM((tokens, width), bf16),
                pltpu.VMEM((tokens, width), bf16),
                pltpu.VMEM((groups, taps), f32),
                pltpu.VMEM(norm_gain.shape, f32),
                pltpu.VMEM(doc_ids.shape, jnp.int32),
                pltpu.VMEM((2 * tokens, width), bf16),
                pltpu.VMEM((tokens, width), bf16),
                pltpu.VMEM((tokens, width), bf16),
                pltpu.VMEM((most, width), f32),
                pltpu.VMEM((tokens, 2 * tokens), bf16),
                pltpu.VMEM((tokens, LANES), f32),
                pltpu.VMEM((8, width), f32),
                pltpu.VMEM((1, width), f32),
                pltpu.VMEM((n_ctx, 1, width), f32),
                pltpu.SemaphoreType.DMA((3, count)),
                pltpu.SemaphoreType.DMA((count,)),
                pltpu.SemaphoreType.DMA((count,)),
                pltpu.SemaphoreType.DMA((count,)),
                pltpu.SemaphoreType.DMA((count,)),
                pltpu.SemaphoreType.DMA((n_ctx,)),
                pltpu.SemaphoreType.DMA((n_ctx,)),
                pltpu.SemaphoreType.REGULAR((2,)),
            ],
            compiler_params=pltpu.CompilerParams(
                collective_id=0, has_side_effects=True, vmem_limit_bytes=60 << 20
            ),
        )(*[
            pltpu.with_memory_space_constraint(x, pltpu.HBM)
            for x in (activations[0], gate_values[0], out_grad[0], filters[0], norm_gain, doc_ids)
        ])
        grad, gain = pl.pallas_call(
            deliver,
            out_shape=(
                jax.ShapeDtypeStruct((tokens, width), bf16),
                jax.ShapeDtypeStruct((1, width), f32),
            ),
            in_specs=[vmem] * 2,
            out_specs=[hbm] * 2,
            scratch_shapes=[pltpu.SemaphoreType.DMA((5,))],
            compiler_params=pltpu.CompilerParams(vmem_limit_bytes=1 << 20),
        )(*[pltpu.with_memory_space_constraint(x, pltpu.VMEM) for x in (grad, gain)])
        return grad[None], gain

    return jax.shard_map(
        on_device,
        mesh=mesh,
        in_specs=(
            P("pipe", "ctx", None),
            P("pipe", "ctx", None),
            P("pipe", "ctx", None),
            P("pipe", None, None),
            P("pipe", None),
            P("pipe", None),
        ),
        out_specs=(P("pipe", "ctx", None), P("pipe", None)),
        check_vma=False,
    )
```
